32 devices in a mesh: group: 2 (over x), date: 16 (over z, y, core).
Axes of the slice: x: 2, y: 2, z: 4, core: 2. Of those that a mesh axis runs over, the one named last changes fastest.
Arguments:
- slc_stack: bfloat16 [16, 2, 32, 16384], P('date', None, 'group'), parts along dimension 2, may hold values from -30 to 30
- band_taps: bfloat16 [2, 2, 32], replicated, may hold values from -1 to 1
- pair_flags: int32 [16, 4], P('date'), may hold values from 0 to 1, as said below
Outputs:
- iono_phase: float32 [16, 8, 1024], P('date', 'group'), parts along dimension 1
- weight_sum: float32 [16, 8, 1024], P('date', 'group'), parts along dimension 1
The draws below stay inside these ranges and needn't reach their ends.
There are 2 independent parts, one for each index of `group`. The reference program is written for one: setup_inputs(seed, part) draws one part's arguments, and reference() takes and returns one part's arrays. A program takes and returns all parts, laid end to end along the dimension named above; an argument that names none is the same for every part. Nothing has to cross between parts.
Inputs may be any that keep to these rules, and one draw needn't show every extreme that they name: pair_flags[d,0] is 1 for every date but the last; pair_flags[d,k] is 0 where d + k + 1 >= 16.
All inputs are finite; a program needn't handle non-finite values.
Results may differ from the reference program's by a relative error of at most 0.002.
Values may be sent and summed in bfloat16 or wider, within the bound.
A program may use at most 128 MiB of HBM per device.

```python
import jax
import jax.numpy as jnp
from jax import lax

ROWS = 16
RANGE = 16384
TAPS = 32
ML_AZ = 4
ML_RG = 16
SPAN = 4
RADIUS = 8
ITERS = 4
DATES = 16
AZ_L = 4
RG_L = 1024


def draw_slc_stack(key, part):
    keys = jax.random.split(jax.random.fold_in(key, 17), 5)
    scenery = jax.random.normal(keys[0], (2, ROWS, RANGE), jnp.float32)
    slopes = jax.random.uniform(keys[1], (DATES, 1, 1), jnp.float32, -3.0, 3.0)
    columns = jnp.arange(RANGE, dtype=jnp.float32)[None, None, :] * (25.0 / RANGE)
    rough = 0.4 * jax.random.normal(keys[2], (DATES, ROWS, RANGE), jnp.float32)
    angles = slopes * columns + rough
    real_part = scenery[0][None] * jnp.cos(angles) - scenery[1][None] * jnp.sin(angles)
    imag_part = scenery[0][None] * jnp.sin(angles) + scenery[1][None] * jnp.cos(angles)
    noise = 0.5 * jax.random.normal(keys[4], (DATES, 2, ROWS, RANGE), jnp.float32)
    result = jnp.stack([real_part, imag_part], axis=1) + noise
    return jnp.clip(result, -30.0, 30.0).astype(jnp.bfloat16)


def draw_pair_flags(key, part):
    flags = jax.random.randint(jax.random.fold_in(key, 29), (DATES, SPAN), 0, 2, jnp.int32)
    column = lax.broadcasted_iota(jnp.int32, (DATES, SPAN), 1)
    date_ids = lax.broadcasted_iota(jnp.int32, (DATES, SPAN), 0)
    flags = jnp.where(column == 0, 1, flags)
    present = (date_ids + column + 1 < DATES).astype(jnp.int32)
    return (flags * present).astype(jnp.int32)


def scatter_about(key, shape, scale, bound, held_as=jnp.bfloat16):
    drawn = scale * jax.random.normal(key, shape, jnp.float32)
    return jnp.clip(drawn, min=-bound, max=bound).astype(held_as)


def setup_inputs(seed: int = 0, part: int = 0) -> dict:
    seeds = jax.random.split(jax.random.key(seed), 4)
    part_splits = jax.random.split(jax.random.fold_in(seeds[3], part), 4)
    return {
        "slc_stack": draw_slc_stack(jax.random.fold_in(jax.random.fold_in(seeds[3], part), 71), part),
        "band_taps": scatter_about(seeds[1], (2, 2, TAPS), TAPS ** -0.5, 1.0),
        "pair_flags": draw_pair_flags(jax.random.fold_in(seeds[3], 71), part),
    }


eps_power = 1e-06
floor_weight = 0.1
ridge_weight = 0.05
split_coef = 2.0

def band_split(one_scene, band_taps):
    signal = one_scene.astype(jnp.float32)
    left_pad = TAPS // 2
    padded = jnp.pad(signal, ((0, 0), (0, 0), (left_pad, TAPS - 1 - left_pad)))
    coeffs = band_taps.astype(jnp.float32)
    result = jnp.zeros((2, 2, ROWS, RANGE), jnp.float32)
    for offset in range(TAPS):
        window = padded[:, :, offset:offset + RANGE]
        real_tap = coeffs[:, 0, offset][:, None, None]
        imag_tap = coeffs[:, 1, offset][:, None, None]
        real_part = real_tap * window[0] - imag_tap * window[1]
        imag_part = imag_tap * window[0] + real_tap * window[1]
        result = result + jnp.stack([real_part, imag_part], axis=1)
    return result.astype(jnp.bfloat16)

def multilook(values):
    shaped = values.reshape(values.shape[:-2] + (AZ_L, ML_AZ, RG_L, ML_RG))
    return shaped.sum(axis=(-3, -1))

def later_of(values, offset):
    return jnp.concatenate([values[offset:], jnp.zeros_like(values[:offset])], axis=0)

def earlier_of(values, offset):
    return jnp.concatenate([jnp.zeros_like(values[:offset]), values[:-offset]], axis=0)

def reference(slc_stack, band_taps, pair_flags):
    bands = lax.map(lambda one_scene: band_split(one_scene, band_taps), slc_stack)

    def power_of(piece):
        values = piece.astype(jnp.float32)
        return multilook(values[:, 0] * values[:, 0] + values[:, 1] * values[:, 1])
    powers = lax.map(power_of, bands)
    date_ids = jnp.arange(DATES, dtype=jnp.int32)

    def pair_of(date_index):
        own_bands = lax.dynamic_index_in_dim(bands, date_index, 0, keepdims=False).astype(jnp.float32)
        real_list = []
        imag_list = []
        for offset in range(1, SPAN + 1):
            other_index = jnp.minimum(date_index + offset, DATES - 1).astype(jnp.int32)
            present = (date_index + offset < DATES).astype(jnp.float32)
            partner = lax.dynamic_index_in_dim(bands, other_index, 0, keepdims=False).astype(jnp.float32) * present
            real_part = own_bands[:, 0] * partner[:, 0] + own_bands[:, 1] * partner[:, 1]
            imag_part = own_bands[:, 1] * partner[:, 0] - own_bands[:, 0] * partner[:, 1]
            real_list.append(multilook(real_part))
            imag_list.append(multilook(imag_part))
        return (jnp.stack(real_list, axis=0), jnp.stack(imag_list, axis=0))
    cross_real, cross_imag = lax.map(pair_of, date_ids)
    partner_power = jnp.stack([later_of(powers, offset) for offset in range(1, SPAN + 1)], axis=1)
    own_power = powers[:, None]
    coherence = (cross_real ** 2 + cross_imag ** 2) / (own_power * partner_power + eps_power)
    flags = pair_flags.astype(jnp.float32)[:, :, None, None]
    weight = flags * 0.5 * (coherence[:, :, 0] + coherence[:, :, 1])
    normalizer = jnp.sqrt((own_power[:, :, 0] * partner_power[:, :, 0] + eps_power) * (own_power[:, :, 1] * partner_power[:, :, 1] + eps_power))
    cross_term = cross_imag[:, :, 0] * cross_real[:, :, 1] - cross_real[:, :, 0] * cross_imag[:, :, 1]
    raw_phase = split_coef * cross_term / normalizer
    row_ids = lax.broadcasted_iota(jnp.int32, (RG_L, RG_L), 0)
    col_ids = lax.broadcasted_iota(jnp.int32, (RG_L, RG_L), 1)
    box_matrix = (jnp.abs(row_ids - col_ids) <= RADIUS).astype(jnp.float32)
    numerator = jnp.matmul(weight * raw_phase, box_matrix, precision=lax.Precision.HIGHEST)
    denominator = jnp.matmul(weight, box_matrix, precision=lax.Precision.HIGHEST)
    pair_phase = numerator / (denominator + floor_weight)
    smooth_weight = denominator / (2 * RADIUS + 1)
    first_pair = pair_phase[:, 0]
    chain_start = jnp.cumsum(jnp.concatenate([jnp.zeros_like(first_pair[:1]), first_pair[:-1]], axis=0), axis=0)
    low_weight = [earlier_of(smooth_weight[:, offset - 1], offset) for offset in range(1, SPAN + 1)]
    low_phase = [earlier_of(pair_phase[:, offset - 1], offset) for offset in range(1, SPAN + 1)]
    weight_sum = jnp.zeros_like(chain_start)
    for offset in range(1, SPAN + 1):
        weight_sum = weight_sum + smooth_weight[:, offset - 1] + low_weight[offset - 1]
    diagonal = weight_sum + ridge_weight
    iono_phase = chain_start
    for sweep_index in range(ITERS):
        accumulated = ridge_weight * chain_start
        for offset in range(1, SPAN + 1):
            accumulated = accumulated + smooth_weight[:, offset - 1] * (later_of(iono_phase, offset) - pair_phase[:, offset - 1])
            accumulated = accumulated + low_weight[offset - 1] * (earlier_of(iono_phase, offset) + low_phase[offset - 1])
        iono_phase = accumulated / diagonal
    return (iono_phase, weight_sum)
```

```python
import functools

import jax
import jax.numpy as jnp
from jax import lax
from jax.experimental import pallas as pl
from jax.experimental.pallas import tpu as pltpu
from jax.sharding import PartitionSpec as P

TAPS = 32
ML_AZ = 4
ML_RG = 16
SPAN = 4
RADIUS = 8
ITERS = 4

LANES = 128
CELLS = LANES // ML_RG

eps_power = 1e-06
floor_weight = 0.1
ridge_weight = 0.05
split_coef = 2.0

F32 = jnp.float32
BF16 = jnp.bfloat16


def kernel(
    n, n_rg, pieces,
    data_ref, flags_ref, taps_ref, out_ref,
    recv, flags, mat, filt, bands, power, raw_w, raw_n, wgt, phs, phi_a, phi_b,
    rhs, inv, wsum, pack, back,
    send_sem, recv_sem, fsend_sem, frecv_sem, osend_sem, orecv_sem,
):
    me = lax.axis_index("date")
    blocks = pieces - 1
    own_blocks = pieces - 4
    rows_pad = bands.shape[2]
    my_q = lax.rem(me, n_rg)

    barrier = pltpu.get_barrier_semaphore()

    def greet(i, carry):
        other = lax.rem(me + i, n)
        pl.semaphore_signal(
            barrier, inc=1, device_id={"date": other}, device_id_type=pl.DeviceIdType.MESH
        )
        return carry

    lax.fori_loop(1, n, greet, 0)

    own_copy = pltpu.make_async_copy(data_ref.at[me], recv.at[me], recv_sem.at[me])
    own_copy.start()
    own_flags = pltpu.make_async_copy(flags_ref, flags.at[me + SPAN], frecv_sem.at[me])
    own_flags.start()

    pl.semaphore_wait(barrier, n - 1)

    def data_copy(target, slot):
        return pltpu.make_async_remote_copy(
            src_ref=data_ref.at[target], dst_ref=recv.at[me],
            send_sem=send_sem.at[target], recv_sem=recv_sem.at[me],
            device_id={"date": target}, device_id_type=pl.DeviceIdType.MESH,
        )

    def flag_copy(target):
        return pltpu.make_async_remote_copy(
            src_ref=flags_ref, dst_ref=flags.at[me + SPAN],
            send_sem=fsend_sem.at[target], recv_sem=frecv_sem.at[me],
            device_id={"date": target}, device_id_type=pl.DeviceIdType.MESH,
        )

    def send(i, carry):
        target = lax.rem(me + i, n)
        flag_copy(target).start()
        data_copy(target, 0).start()
        return carry

    lax.fori_loop(1, n, send, 0)

    k_id = lax.broadcasted_iota(jnp.int32, (LANES, LANES), 0)
    j_id = lax.broadcasted_iota(jnp.int32, (LANES, LANES), 1)
    circ = []
    for m in range(4):
        base = jnp.broadcast_to(taps_ref[m:m + 1, :], (LANES, LANES))
        circ.append(pltpu.roll(base, 0, 1, stride=1, stride_axis=0))
    for half in range(2):
        keep = (j_id <= k_id) if half == 0 else (j_id > k_id)
        for band in range(2):
            re_part = jnp.where(keep, circ[2 * band], 0.0).astype(BF16)
            im_value = jnp.where(keep, circ[2 * band + 1], 0.0)
            im_part = im_value.astype(BF16)
            im_minus = (-im_value).astype(BF16)
            col = half * 512 + band * 256
            mat[0:128, col:col + 128] = re_part
            mat[0:128, col + 128:col + 256] = im_part
            mat[128:256, col:col + 128] = im_minus
            mat[128:256, col + 128:col + 256] = re_part

    for ref in (bands, power, raw_w, raw_n, wgt, phs, phi_a, phi_b):
        ref[...] = jnp.zeros_like(ref)
    flags[0:SPAN] = jnp.zeros((SPAN,) + flags.shape[1:], F32)

    cell_row = lax.broadcasted_iota(jnp.int32, (CELLS, 4 * LANES), 0)
    lane = lax.broadcasted_iota(jnp.int32, (CELLS, 4 * LANES), 1)
    pick = lax.rem(lane, LANES) // ML_RG == cell_row
    sum_re = jnp.where(pick, 1.0, 0.0).astype(BF16)
    sum_im = jnp.where(pick, jnp.where(lax.rem(lane, 2 * LANES) < LANES, -1.0, 1.0), 0.0).astype(BF16)
    contract = (((1,), (1,)), ((), ()))

    def looks(value, selector):
        high = value.astype(BF16)
        low = (value - high.astype(F32)).astype(BF16)
        both = jnp.concatenate([high, low], axis=1)
        return lax.dot_general(selector, both, contract, preferred_element_type=F32)

    ring = bands.shape[0]

    def one_date(d, carry):
        pltpu.make_async_copy(recv.at[d], recv.at[d], recv_sem.at[d]).wait()
        pltpu.make_async_copy(
            flags.at[d + SPAN], flags.at[d + SPAN], frecv_sem.at[d]
        ).wait()
        filt[...] = jnp.dot(recv[d], mat[...], preferred_element_type=F32)
        slot = lax.rem(d, ring)
        for r in range(ML_AZ):
            first = r * pieces
            value = filt[first:first + blocks, 0:512] + filt[first + 1:first + 1 + blocks, 512:1024]
            bands[slot, r, 0:blocks, :] = value.astype(BF16).astype(F32)
        new_power = []
        for band in range(2):
            total = None
            for r in range(ML_AZ):
                value = bands[slot, r, :, band * 256:band * 256 + 256]
                total = value * value if total is None else total + value * value
            new_power.append(looks(total, sum_re))
            power[slot, band, :, 0:rows_pad] = new_power[band]
        for k in range(1, SPAN + 1):
            early = lax.rem(d + ring - k, ring)
            cross = []
            for band in range(2):
                total_re = None
                total_im = None
                for r in range(ML_AZ):
                    a = bands[early, r, :, band * 256:band * 256 + 256]
                    b = bands[slot, r, :, band * 256:band * 256 + 256]
                    b_swap = jnp.concatenate([b[:, 128:], b[:, :128]], axis=1)
                    total_re = a * b if total_re is None else total_re + a * b
                    total_im = a * b_swap if total_im is None else total_im + a * b_swap
                cross.append((looks(total_re, sum_re), looks(total_im, sum_im)))
            (cr0, ci0), (cr1, ci1) = cross
            ab0 = power[early, 0, :, 0:rows_pad] * new_power[0] + eps_power
            ab1 = power[early, 1, :, 0:rows_pad] * new_power[1] + eps_power
            flag = flags[d - k + SPAN, k - 1:k, 0:rows_pad]
            weight = flag * 0.5 * ((cr0 * cr0 + ci0 * ci0) / ab0 + (cr1 * cr1 + ci1 * ci1) / ab1)
            phase = split_coef * (ci0 * cr1 - cr0 * ci1) / jnp.sqrt(ab0 * ab1)
            raw_w[k - 1, d - k + SPAN, :, 0:rows_pad] = weight
            raw_n[k - 1, d - k + SPAN, :, 0:rows_pad] = weight * phase
        return carry

    lax.fori_loop(0, n, one_date, 0)

    step = min(8, n)
    shape = (step, CELLS, LANES)
    c_id = lax.broadcasted_iota(jnp.int32, shape, 1)
    b_id = lax.broadcasted_iota(jnp.int32, shape, 2)
    cell = CELLS * (own_blocks * my_q - 2 + b_id) + 1 + c_id
    valid = (b_id < blocks) & (cell >= 0) & (cell < n_rg * own_blocks * CELLS)

    def box(value):
        value = jnp.where(valid, value, 0.0)
        prefix = value
        for hop in (1, 2, 4):
            prefix = prefix + jnp.where(c_id >= hop, pltpu.roll(prefix, hop, 1), 0.0)
        whole = jnp.sum(value, axis=1, keepdims=True)
        suffix = whole - prefix + value
        return pltpu.roll(suffix, 1, 2) + whole + pltpu.roll(prefix, LANES - 1, 2)

    def smooth(i, carry):
        at = i * step + SPAN
        for k in range(SPAN):
            den = box(raw_w[k, pl.ds(at, step)])
            num = box(raw_n[k, pl.ds(at, step)])
            phs[k, pl.ds(at, step)] = num / (den + floor_weight)
            wgt[k, pl.ds(at, step)] = den / (2 * RADIUS + 1)
        return carry

    lax.fori_loop(0, n // step, smooth, 0)

    def chain(d, state):
        phi_a[d + SPAN] = state
        return state + phs[0, d + SPAN]

    lax.fori_loop(0, n, chain, jnp.zeros((CELLS, LANES), F32))

    def constants(i, carry):
        at = i * step + SPAN
        total = jnp.zeros(shape, F32)
        acc = ridge_weight * phi_a[pl.ds(at, step)]
        for k in range(1, SPAN + 1):
            w = wgt[k - 1, pl.ds(at, step)]
            low = wgt[k - 1, pl.ds(at - k, step)]
            total = total + w + low
            acc = acc - w * phs[k - 1, pl.ds(at, step)] + low * phs[k - 1, pl.ds(at - k, step)]
        wsum[pl.ds(i * step, step)] = total
        rhs[pl.ds(i * step, step)] = acc
        inv[pl.ds(i * step, step)] = 1.0 / (total + ridge_weight)
        return carry

    lax.fori_loop(0, n // step, constants, 0)

    for sweep in range(ITERS):
        old, new = (phi_a, phi_b) if sweep % 2 == 0 else (phi_b, phi_a)

        def relax(i, carry):
            at = i * step + SPAN
            acc = rhs[pl.ds(i * step, step)]
            for k in range(1, SPAN + 1):
                acc = acc + wgt[k - 1, pl.ds(at, step)] * old[pl.ds(at + k, step)]
                acc = acc + wgt[k - 1, pl.ds(at - k, step)] * old[pl.ds(at - k, step)]
            new[pl.ds(at, step)] = acc * inv[pl.ds(i * step, step)]
            return carry

        lax.fori_loop(0, n // step, relax, 0)
    last = phi_a if ITERS % 2 == 0 else phi_b

    def align(value):
        down = pltpu.roll(value, 1, 1)
        return jnp.where(c_id == 0, pltpu.roll(down, LANES - 1, 2), pltpu.roll(down, LANES - 2, 2))

    def finish(i, carry):
        phase = align(last[pl.ds(i * step + SPAN, step)])
        total = align(wsum[pl.ds(i * step, step)])
        pack[pl.ds(i * step, step)] = jnp.where(b_id < 64, phase, pltpu.roll(total, 64, 2))
        return carry

    lax.fori_loop(0, n // step, finish, 0)

    def out_copy(target):
        return pltpu.make_async_remote_copy(
            src_ref=pack.at[target], dst_ref=back.at[me],
            send_sem=osend_sem.at[target], recv_sem=orecv_sem.at[me],
            device_id={"date": target}, device_id_type=pl.DeviceIdType.MESH,
        )

    own_back = pltpu.make_async_copy(pack.at[me], back.at[me], orecv_sem.at[me])
    own_back.start()

    def send_back(i, carry):
        out_copy(lax.rem(me + i, n)).start()
        return carry

    lax.fori_loop(1, n, send_back, 0)

    def drain(i, carry):
        target = lax.rem(me + i, n)
        data_copy(target, 0).wait_send()
        flag_copy(target).wait_send()
        out_copy(target).wait_send()
        return carry

    lax.fori_loop(1, n, drain, 0)

    def arrive(s, carry):
        pltpu.make_async_copy(back.at[s], back.at[s], orecv_sem.at[s]).wait()
        out_ref[s] = back[s]
        return carry

    lax.fori_loop(0, n, arrive, 0)


def local(slc_stack, band_taps, pair_flags):
    n = lax.axis_size("date")
    rows, span = slc_stack.shape[2:]
    n_az = rows // ML_AZ
    n_rg = n // n_az
    own_blocks = span // LANES // n_rg
    pieces = own_blocks + 4
    rows_pad = -(-(pieces - 1) // 8) * 8
    chunk_rows = ML_AZ * pieces

    x = slc_stack[0].reshape(2, n_az, ML_AZ, span // LANES, LANES).transpose(1, 2, 3, 0, 4)
    x = jnp.pad(x, ((0, 0), (0, 0), (2, 2), (0, 0), (0, 0)))
    chunks = [x[:, :, q * own_blocks:q * own_blocks + pieces] for q in range(n_rg)]
    data = jnp.stack(chunks, axis=1).reshape(n, chunk_rows, 2 * LANES)

    flags = jnp.broadcast_to(
        jnp.pad(pair_flags[0].astype(F32), (0, 8 - SPAN))[:, None], (8, LANES)
    )
    h = band_taps.astype(F32).reshape(4, TAPS)
    taps = jnp.concatenate(
        [h[:, :1], jnp.zeros((4, LANES - TAPS), F32), jnp.flip(h[:, 1:], axis=1)], axis=1
    )
    taps = jnp.pad(taps, ((0, 4), (0, 0)))

    vmem = pl.BlockSpec(memory_space=pltpu.VMEM)
    small = lambda *lead: pltpu.VMEM((*lead, CELLS, LANES), F32)
    ring = SPAN + 1
    sem = pltpu.SemaphoreType.DMA((n,))
    back = pl.pallas_call(
        functools.partial(kernel, n, n_rg, pieces),
        out_shape=jax.ShapeDtypeStruct((n, CELLS, LANES), F32),
        in_specs=[vmem] * 3,
        out_specs=vmem,
        scratch_shapes=[
            pltpu.VMEM((n, chunk_rows, 2 * LANES), BF16),
            small(n + SPAN),
            pltpu.VMEM((256, 1024), BF16),
            pltpu.VMEM((chunk_rows, 1024), F32),
            pltpu.VMEM((ring, ML_AZ, rows_pad, 512), F32),
            small(ring, 2),
            small(SPAN, n + 2 * SPAN),
            small(SPAN, n + 2 * SPAN),
            small(SPAN, n + 2 * SPAN),
            small(SPAN, n + 2 * SPAN),
            small(n + 2 * SPAN),
            small(n + 2 * SPAN),
            small(n),
            small(n),
            small(n),
            small(n),
            small(n),
            sem, sem, sem, sem, sem, sem,
        ],
        compiler_params=pltpu.CompilerParams(
            collective_id=0, has_side_effects=True, vmem_limit_bytes=48 * 1024 * 1024
        ),
    )(data, flags, taps)
    outs = back.reshape(n_az, n_rg, CELLS, 2, LANES // 2)[..., :own_blocks]
    outs = outs.transpose(3, 0, 1, 4, 2).reshape(2, 1, n_az, span // ML_RG)
    return outs[0], outs[1]


def solution(mesh):
    in_specs = (P("date", None, "group", None), P(), P("date", None))
    out_specs = (P("date", "group", None), P("date", "group", None))
    return jax.shard_map(local, mesh=mesh, in_specs=in_specs, out_specs=out_specs, check_vma=False)
```

```python
import functools

import jax
import jax.numpy as jnp
from jax import lax
from jax.experimental import pallas as pl
from jax.experimental.pallas import tpu as pltpu
from jax.sharding import PartitionSpec as P

TAPS = 32
ML_AZ = 4
ML_RG = 16
SPAN = 4
RADIUS = 8
ITERS = 4

LANES = 128
CELLS = LANES // ML_RG

eps_power = 1e-06
floor_weight = 0.1
ridge_weight = 0.05
split_coef = 2.0

F32 = jnp.float32
BF16 = jnp.bfloat16


def kernel(
    n, n_rg, pieces, cuts,
    slc_ref, flags_in, taps_ref, out_ref,
    slc, data, own_flags, recv, flags, mat, filt, bands, power, raw_w, raw_n, wgt, phs, phi_a, phi_b,
    rhs, inv, wsum, pack, back,
    in_sem, send_sem, recv_sem, fsend_sem, frecv_sem, osend_sem, orecv_sem,
):
    me = lax.axis_index("date")
    blocks = pieces - 1
    own_blocks = pieces - 4
    rows_pad = bands.shape[2]
    my_q = lax.rem(me, n_rg)

    barrier = pltpu.get_barrier_semaphore()

    def greet(i, carry):
        other = lax.rem(me + i, n)
        pl.semaphore_signal(
            barrier, inc=1, device_id={"date": other}, device_id_type=pl.DeviceIdType.MESH
        )
        return carry

    lax.fori_loop(1, n, greet, 0)

    load = pltpu.make_async_copy(slc_ref.at[0], slc, in_sem)
    load.start()

    row_8 = lax.broadcasted_iota(jnp.int32, (8, 4), 0)
    col_8 = lax.broadcasted_iota(jnp.int32, (8, 4), 1)
    picked = jnp.where(row_8 == col_8, flags_in[...].astype(F32), 0.0)
    own_flags[...] = jnp.broadcast_to(jnp.sum(picked, axis=1, keepdims=True), (8, LANES))
    load.wait()

    n_az = n // n_rg
    n_tiles = data.shape[1] // 16
    n_blocks = slc.shape[2] // LANES
    upper = lax.broadcasted_iota(jnp.int32, (8, LANES), 0) < ML_AZ

    def regroup(tile, lo, hi):
        for part in range(2):
            for half in range(n_az // 2):
                made = ([], [])
                for pair in range(2):
                    two = []
                    for m in (2 * pair, 2 * pair + 1):
                        if lo <= m < hi:
                            at = pl.multiple_of((4 * tile - 2 + m) * LANES, LANES)
                            value = slc[part, :, pl.ds(at, LANES)].astype(F32)
                            two.append(value[8 * half:8 * half + 8])
                        else:
                            two.append(jnp.zeros((8, LANES), F32))
                    made[0].append(jnp.where(upper, two[0], pltpu.roll(two[1], ML_AZ, 0)))
                    made[1].append(jnp.where(upper, pltpu.roll(two[0], ML_AZ, 0), two[1]))
                for odd in range(2):
                    value = jnp.concatenate(made[odd], axis=0).astype(BF16)
                    to = pl.multiple_of(tile * 16, 16)
                    data[2 * half + odd, pl.ds(to, 16), part * LANES:part * LANES + LANES] = value

    def inner_tile(tile, carry):
        regroup(tile, 0, 4)
        return carry

    lax.fori_loop(1, n_tiles - 1, inner_tile, 0, unroll=False)
    regroup(0, 2, 4)
    regroup(n_tiles - 1, 0, 2)

    chunk_rows = ML_AZ * pieces
    stride_rows = ML_AZ * own_blocks

    def strip_of(ref, strip):
        lo, hi = cuts[strip], cuts[strip + 1]
        return ref.at[pl.ds(lo, hi - lo)]

    def source(target, strip):
        lo, hi = cuts[strip], cuts[strip + 1]
        begin = pl.multiple_of(lax.rem(target, n_rg) * stride_rows + lo, 16)
        return data.at[target // n_rg, pl.ds(begin, hi - lo)]

    def data_copy(target, strip):
        return pltpu.make_async_remote_copy(
            src_ref=source(target, strip), dst_ref=strip_of(recv.at[me], strip),
            send_sem=send_sem.at[strip, target], recv_sem=recv_sem.at[strip, me],
            device_id={"date": target}, device_id_type=pl.DeviceIdType.MESH,
        )

    def flag_copy(target):
        return pltpu.make_async_remote_copy(
            src_ref=own_flags, dst_ref=flags.at[me + SPAN],
            send_sem=fsend_sem.at[target], recv_sem=frecv_sem.at[me],
            device_id={"date": target}, device_id_type=pl.DeviceIdType.MESH,
        )

    for strip in range(2):
        pltpu.make_async_copy(
            source(me, strip), strip_of(recv.at[me], strip), recv_sem.at[strip, me]
        ).start()
    pltpu.make_async_copy(own_flags, flags.at[me + SPAN], frecv_sem.at[me]).start()

    pl.semaphore_wait(barrier, n - 1)

    def send_first(i, carry):
        target = lax.rem(me + i, n)
        data_copy(target, 0).start()
        flag_copy(target).start()
        return carry

    lax.fori_loop(1, n, send_first, 0)

    def send_second(i, carry):
        data_copy(lax.rem(me + i, n), 1).start()
        return carry

    lax.fori_loop(1, n, send_second, 0)

    k_id = lax.broadcasted_iota(jnp.int32, (LANES, LANES), 0)
    j_id = lax.broadcasted_iota(jnp.int32, (LANES, LANES), 1)
    circ = []
    for m in range(4):
        base = jnp.broadcast_to(taps_ref[m:m + 1, :], (LANES, LANES))
        circ.append(pltpu.roll(base, 0, 1, stride=1, stride_axis=0).T)
    for half in range(2):
        keep = (j_id <= k_id) if half == 0 else (j_id > k_id)
        for band in range(2):
            re_part = jnp.where(keep, circ[2 * band], 0.0).astype(BF16)
            im_value = jnp.where(keep, circ[2 * band + 1], 0.0)
            im_part = im_value.astype(BF16)
            im_minus = (-im_value).astype(BF16)
            col = half * 512 + band * 256
            mat[0:128, col:col + 128] = re_part
            mat[0:128, col + 128:col + 256] = im_part
            mat[128:256, col:col + 128] = im_minus
            mat[128:256, col + 128:col + 256] = re_part

    for ref in (raw_w, raw_n, wgt, phs, phi_a, phi_b):
        ref[...] = jnp.zeros_like(ref)
    flags[0:SPAN] = jnp.zeros((SPAN,) + flags.shape[1:], F32)

    cell_row = lax.broadcasted_iota(jnp.int32, (CELLS, 4 * LANES), 0)
    lane = lax.broadcasted_iota(jnp.int32, (CELLS, 4 * LANES), 1)
    pick = lax.rem(lane, LANES) // ML_RG == cell_row
    sum_re = jnp.where(pick, 1.0, 0.0).astype(BF16)
    sum_im = jnp.where(pick, jnp.where(lax.rem(lane, 2 * LANES) < LANES, -1.0, 1.0), 0.0).astype(BF16)
    contract = (((1,), (1,)), ((), ()))

    def looks(value, selector):
        high = value.astype(BF16)
        low = (value - high.astype(F32)).astype(BF16)
        both = jnp.concatenate([high, low], axis=1)
        return lax.dot_general(selector, both, contract, preferred_element_type=F32)

    ring = bands.shape[0]

    def one_date(strip, d):
        r0, r1 = cuts[strip], cuts[strip + 1]
        first = max(r0 - ML_AZ, 0)
        b0 = first // ML_AZ
        count = (r1 - first) // ML_AZ - 1
        pad = -(-count // 8) * 8
        pltpu.make_async_copy(
            strip_of(recv.at[d], strip), strip_of(recv.at[d], strip), recv_sem.at[strip, d]
        ).wait()
        if strip == 0:
            pltpu.make_async_copy(
                flags.at[d + SPAN], flags.at[d + SPAN], frecv_sem.at[d]
            ).wait()
        base = first // 16 * 16
        off = first - base
        made = jnp.dot(recv[d, base:r1], mat[...], preferred_element_type=F32)
        for g in range(8):
            filt[g, 0:r1 - base, :] = made[:, g * LANES:g * LANES + LANES]
        slot = lax.rem(d, ring)
        for r in range(ML_AZ):
            for g in range(4):
                low = filt[g, pl.ds(off + r, count, stride=ML_AZ), :]
                high = filt[g + 4, pl.ds(off + r + ML_AZ, count, stride=ML_AZ), :]
                value = (low + high).astype(BF16).astype(F32)
                bands[slot, r, 0:count, g * LANES:g * LANES + LANES] = value
        new_power = []
        for band in range(2):
            total = None
            for r in range(ML_AZ):
                value = bands[slot, r, 0:pad, band * 256:band * 256 + 256]
                total = value * value if total is None else total + value * value
            new_power.append(looks(total, sum_re))
            power[slot, band, :, 0:pad] = new_power[band]
        for k in range(1, SPAN + 1):
            early = lax.rem(d + ring - k, ring)
            cross = []
            for band in range(2):
                total_re = None
                total_im = None
                for r in range(ML_AZ):
                    a = bands[early, r, 0:pad, band * 256:band * 256 + 256]
                    b = bands[slot, r, 0:pad, band * 256:band * 256 + 256]
                    b_swap = jnp.concatenate([b[:, 128:], b[:, :128]], axis=1)
                    total_re = a * b if total_re is None else total_re + a * b
                    total_im = a * b_swap if total_im is None else total_im + a * b_swap
                cross.append((looks(total_re, sum_re), looks(total_im, sum_im)))
            (cr0, ci0), (cr1, ci1) = cross
            ab0 = power[early, 0, :, 0:pad] * new_power[0] + eps_power
            ab1 = power[early, 1, :, 0:pad] * new_power[1] + eps_power
            flag = flags[d - k + SPAN, k - 1:k, 0:pad]
            weight = flag * 0.5 * ((cr0 * cr0 + ci0 * ci0) / ab0 + (cr1 * cr1 + ci1 * ci1) / ab1)
            phase = split_coef * (ci0 * cr1 - cr0 * ci1) / jnp.sqrt(ab0 * ab1)
            raw_w[k - 1, d - k + SPAN, :, b0:b0 + count] = weight[:, 0:count]
            raw_n[k - 1, d - k + SPAN, :, b0:b0 + count] = (weight * phase)[:, 0:count]

    for strip in range(2):
        bands[...] = jnp.zeros_like(bands)
        power[...] = jnp.zeros_like(power)

        def step_date(d, carry):
            one_date(strip, d)
            return carry

        lax.fori_loop(0, n, step_date, 0)

    step = min(8, n)
    shape = (step, CELLS, LANES)
    c_id = lax.broadcasted_iota(jnp.int32, shape, 1)
    b_id = lax.broadcasted_iota(jnp.int32, shape, 2)
    cell = CELLS * (own_blocks * my_q - 2 + b_id) + 1 + c_id
    valid = (b_id < blocks) & (cell >= 0) & (cell < n_rg * own_blocks * CELLS)

    def box(value):
        value = jnp.where(valid, value, 0.0)
        prefix = value
        for hop in (1, 2, 4):
            prefix = prefix + jnp.where(c_id >= hop, pltpu.roll(prefix, hop, 1), 0.0)
        whole = jnp.sum(value, axis=1, keepdims=True)
        suffix = whole - prefix + value
        return pltpu.roll(suffix, 1, 2) + whole + pltpu.roll(prefix, LANES - 1, 2)

    def smooth(i, carry):
        at = i * step + SPAN
        for k in range(SPAN):
            den = box(raw_w[k, pl.ds(at, step)])
            num = box(raw_n[k, pl.ds(at, step)])
            phs[k, pl.ds(at, step)] = num / (den + floor_weight)
            wgt[k, pl.ds(at, step)] = den / (2 * RADIUS + 1)
        return carry

    lax.fori_loop(0, n // step, smooth, 0)

    def chain(d, state):
        phi_a[d + SPAN] = state
        return state + phs[0, d + SPAN]

    lax.fori_loop(0, n, chain, jnp.zeros((CELLS, LANES), F32))

    def constants(i, carry):
        at = i * step + SPAN
        total = jnp.zeros(shape, F32)
        acc = ridge_weight * phi_a[pl.ds(at, step)]
        for k in range(1, SPAN + 1):
            w = wgt[k - 1, pl.ds(at, step)]
            low = wgt[k - 1, pl.ds(at - k, step)]
            total = total + w + low
            acc = acc - w * phs[k - 1, pl.ds(at, step)] + low * phs[k - 1, pl.ds(at - k, step)]
        wsum[pl.ds(i * step, step)] = total
        rhs[pl.ds(i * step, step)] = acc
        inv[pl.ds(i * step, step)] = 1.0 / (total + ridge_weight)
        return carry

    lax.fori_loop(0, n // step, constants, 0)

    for sweep in range(ITERS):
        old, new = (phi_a, phi_b) if sweep % 2 == 0 else (phi_b, phi_a)

        def relax(i, carry):
            at = i * step + SPAN
            acc = rhs[pl.ds(i * step, step)]
            for k in range(1, SPAN + 1):
                acc = acc + wgt[k - 1, pl.ds(at, step)] * old[pl.ds(at + k, step)]
                acc = acc + wgt[k - 1, pl.ds(at - k, step)] * old[pl.ds(at - k, step)]
            new[pl.ds(at, step)] = acc * inv[pl.ds(i * step, step)]
            return carry

        lax.fori_loop(0, n // step, relax, 0)
    last = phi_a if ITERS % 2 == 0 else phi_b

    def align(value):
        down = pltpu.roll(value, 1, 1)
        return jnp.where(c_id == 0, pltpu.roll(down, LANES - 1, 2), pltpu.roll(down, LANES - 2, 2))

    def finish(i, carry):
        phase = align(last[pl.ds(i * step + SPAN, step)])
        total = align(wsum[pl.ds(i * step, step)])
        pack[pl.ds(i * step, step)] = jnp.where(b_id < 64, phase, pltpu.roll(total, 64, 2))
        return carry

    lax.fori_loop(0, n // step, finish, 0)

    def out_copy(target):
        return pltpu.make_async_remote_copy(
            src_ref=pack.at[target], dst_ref=back.at[me],
            send_sem=osend_sem.at[target], recv_sem=orecv_sem.at[me],
            device_id={"date": target}, device_id_type=pl.DeviceIdType.MESH,
        )

    own_back = pltpu.make_async_copy(pack.at[me], back.at[me], orecv_sem.at[me])
    own_back.start()

    def send_back(i, carry):
        out_copy(lax.rem(me + i, n)).start()
        return carry

    lax.fori_loop(1, n, send_back, 0)

    def drain(i, carry):
        target = lax.rem(me + i, n)
        data_copy(target, 0).wait_send()
        data_copy(target, 1).wait_send()
        flag_copy(target).wait_send()
        out_copy(target).wait_send()
        return carry

    lax.fori_loop(1, n, drain, 0)

    def arrive(s, carry):
        pltpu.make_async_copy(back.at[s], back.at[s], orecv_sem.at[s]).wait()
        out_ref[s] = back[s]
        return carry

    lax.fori_loop(0, n, arrive, 0)


def local(slc_stack, band_taps, pair_flags):
    n = lax.axis_size("date")
    rows, span = slc_stack.shape[2:]
    n_az = rows // ML_AZ
    n_rg = n // n_az
    own_blocks = span // LANES // n_rg
    pieces = own_blocks + 4
    rows_pad = -(-(pieces - 1) // 8) * 8
    chunk_rows = ML_AZ * pieces

    half = -(-chunk_rows // 32) * 16
    cuts = (0, half, chunk_rows)
    taps = jnp.pad(band_taps.astype(F32).reshape(4, TAPS), ((0, 4), (0, LANES - TAPS)))
    padded_rows = ML_AZ * (span // LANES + 4)

    vmem = pl.BlockSpec(memory_space=pltpu.VMEM)
    small = lambda *lead: pltpu.VMEM((*lead, CELLS, LANES), F32)
    ring = SPAN + 1
    sem = pltpu.SemaphoreType.DMA((n,))
    two_sem = pltpu.SemaphoreType.DMA((2, n))
    back = pl.pallas_call(
        functools.partial(kernel, n, n_rg, pieces, cuts),
        out_shape=jax.ShapeDtypeStruct((n, CELLS, LANES), F32),
        in_specs=[pl.BlockSpec(memory_space=pl.ANY), vmem, vmem],
        out_specs=vmem,
        scratch_shapes=[
            pltpu.VMEM((2, rows, span), BF16),
            pltpu.VMEM((n_az, padded_rows, 2 * LANES), BF16),
            pltpu.VMEM((8, LANES), F32),
            pltpu.VMEM((n, chunk_rows, 2 * LANES), BF16),
            small(n + SPAN),
            pltpu.VMEM((256, 1024), BF16),
            pltpu.VMEM((8, chunk_rows, LANES), F32),
            pltpu.VMEM((ring, ML_AZ, rows_pad, 512), F32),
            small(ring, 2),
            small(SPAN, n + 2 * SPAN),
            small(SPAN, n + 2 * SPAN),
            small(SPAN, n + 2 * SPAN),
            small(SPAN, n + 2 * SPAN),
            small(n + 2 * SPAN),
            small(n + 2 * SPAN),
            small(n),
            small(n),
            small(n),
            small(n),
            small(n),
            pltpu.SemaphoreType.DMA, two_sem, two_sem, sem, sem, sem, sem,
        ],
        compiler_params=pltpu.CompilerParams(
            collective_id=0, has_side_effects=True, vmem_limit_bytes=48 * 1024 * 1024
        ),
    )(slc_stack, pair_flags, taps)
    outs = back.reshape(n_az, n_rg, CELLS, 2, LANES // 2)[..., :own_blocks]
    outs = outs.transpose(3, 0, 1, 4, 2).reshape(2, 1, n_az, span // ML_RG)
    return outs[0], outs[1]


def solution(mesh):
    in_specs = (P("date", None, "group", None), P(), P("date", None))
    out_specs = (P("date", "group", None), P("date", "group", None))
    return jax.shard_map(local, mesh=mesh, in_specs=in_specs, out_specs=out_specs, check_vma=False)
```

```python
import functools

import jax
import jax.numpy as jnp
from jax import lax
from jax.experimental import pallas as pl
from jax.experimental.pallas import tpu as pltpu
from jax.sharding import PartitionSpec as P

TAPS = 32
ML_AZ = 4
ML_RG = 16
SPAN = 4
RADIUS = 8
ITERS = 4

LANES = 128
CELLS = LANES // ML_RG

eps_power = 1e-06
floor_weight = 0.1
ridge_weight = 0.05
split_coef = 2.0

F32 = jnp.float32
BF16 = jnp.bfloat16


def kernel(
    n, n_rg, pieces, cuts,
    slc_hbm, flags_hbm, taps_hbm, phase_out, total_out,
    slc, flags_in, taps_in, taps_ref, data, own_flags, recv, flags, mat, filt, bands, power, cross, wgt, phs, phi_a, phi_b,
    rhs, inv, wsum, pack, back,
    in_sem, send_sem, recv_sem, fsend_sem, frecv_sem, osend_sem, orecv_sem,
):
    me = lax.axis_index("date")
    blocks = pieces - 1
    own_blocks = pieces - 4
    rows_pad = bands.shape[2]
    my_q = lax.rem(me, n_rg)

    slc_load = pltpu.make_async_copy(slc_hbm.at[0], slc, in_sem.at[0])
    slc_load.start()
    flags_load = pltpu.make_async_copy(flags_hbm, flags_in, in_sem.at[1])
    flags_load.start()
    taps_load = pltpu.make_async_copy(taps_hbm, taps_in, in_sem.at[2])
    taps_load.start()
    barrier = pltpu.get_barrier_semaphore()

    def greet(i, carry):
        other = lax.rem(me + i, n)
        pl.semaphore_signal(
            barrier, inc=1, device_id={"date": other}, device_id_type=pl.DeviceIdType.MESH
        )
        return carry

    lax.fori_loop(1, n, greet, 0)

    flags_load.wait()
    own_flags[...] = jnp.zeros_like(own_flags)
    own_flags[0:1, 0:SPAN] = flags_in[...].astype(F32)
    taps_load.wait()
    taps_ref[...] = jnp.zeros_like(taps_ref)
    for band in range(2):
        taps_ref[2 * band:2 * band + 2, 0:TAPS] = taps_in[band].astype(F32)
    slc_load.wait()

    n_az = n // n_rg
    n_tiles = data.shape[1] // 16
    n_blocks = slc.shape[2] // LANES
    upper = lax.broadcasted_iota(jnp.int32, (8, LANES), 0) < ML_AZ

    def regroup(tile, lo, hi):
        for part in range(2):
            for half in range(n_az // 2):
                made = ([], [])
                for pair in range(2):
                    two = []
                    for m in (2 * pair, 2 * pair + 1):
                        if lo <= m < hi:
                            at = pl.multiple_of((4 * tile - 2 + m) * LANES, LANES)
                            value = slc[part, :, pl.ds(at, LANES)].astype(F32)
                            two.append(value[8 * half:8 * half + 8])
                        else:
                            two.append(jnp.zeros((8, LANES), F32))
                    made[0].append(jnp.where(upper, two[0], pltpu.roll(two[1], ML_AZ, 0)))
                    made[1].append(jnp.where(upper, pltpu.roll(two[0], ML_AZ, 0), two[1]))
                for odd in range(2):
                    value = jnp.concatenate(made[odd], axis=0).astype(BF16)
                    to = pl.multiple_of(tile * 16, 16)
                    data[2 * half + odd, pl.ds(to, 16), part * LANES:part * LANES + LANES] = value

    def inner_tile(tile, carry):
        regroup(tile, 0, 4)
        return carry

    lax.fori_loop(1, n_tiles - 1, inner_tile, 0, unroll=False)
    regroup(0, 2, 4)
    regroup(n_tiles - 1, 0, 2)

    chunk_rows = ML_AZ * pieces
    stride_rows = ML_AZ * own_blocks

    def strip_of(ref, strip):
        lo, hi = cuts[strip], cuts[strip + 1]
        return ref.at[pl.ds(lo, hi - lo)]

    def source(target, strip):
        lo, hi = cuts[strip], cuts[strip + 1]
        begin = pl.multiple_of(lax.rem(target, n_rg) * stride_rows + lo, 16)
        return data.at[target // n_rg, pl.ds(begin, hi - lo)]

    def data_copy(target, strip):
        return pltpu.make_async_remote_copy(
            src_ref=source(target, strip), dst_ref=strip_of(recv.at[me], strip),
            send_sem=send_sem.at[strip, target], recv_sem=recv_sem.at[strip, me],
            device_id={"date": target}, device_id_type=pl.DeviceIdType.MESH,
        )

    def flag_copy(target):
        return pltpu.make_async_remote_copy(
            src_ref=own_flags, dst_ref=flags.at[me + SPAN],
            send_sem=fsend_sem.at[target], recv_sem=frecv_sem.at[me],
            device_id={"date": target}, device_id_type=pl.DeviceIdType.MESH,
        )

    for strip in range(2):
        pltpu.make_async_copy(
            source(me, strip), strip_of(recv.at[me], strip), recv_sem.at[strip, me]
        ).start()
    pltpu.make_async_copy(own_flags, flags.at[me + SPAN], frecv_sem.at[me]).start()

    pl.semaphore_wait(barrier, n - 1)

    def send_strip(strip):
        def send_pair(i, carry):
            for target, go in ((n - 1 - i, n - 1 - i > me), (i, i < me)):
                @pl.when(go)
                def _():
                    data_copy(target, strip).start()
                    if strip == 0:
                        flag_copy(target).start()
            return carry

        lax.fori_loop(0, n, send_pair, 0)

    send_strip(0)
    send_strip(1)

    k_id = lax.broadcasted_iota(jnp.int32, (LANES, LANES), 0)
    j_id = lax.broadcasted_iota(jnp.int32, (LANES, LANES), 1)
    circ = []
    for m in range(4):
        base = jnp.broadcast_to(taps_ref[m:m + 1, :], (LANES, LANES))
        circ.append(pltpu.roll(base, 0, 1, stride=1, stride_axis=0).T)
    for half in range(2):
        keep = (j_id <= k_id) if half == 0 else (j_id > k_id)
        for band in range(2):
            re_part = jnp.where(keep, circ[2 * band], 0.0).astype(BF16)
            im_value = jnp.where(keep, circ[2 * band + 1], 0.0)
            im_part = im_value.astype(BF16)
            im_minus = (-im_value).astype(BF16)
            col = half * 512 + band * 256
            mat[0:128, col:col + 128] = re_part
            mat[0:128, col + 128:col + 256] = im_part
            mat[128:256, col:col + 128] = im_minus
            mat[128:256, col + 128:col + 256] = re_part

    for ref in (bands, power, cross, wgt, phs, phi_a, phi_b):
        ref[...] = jnp.zeros_like(ref)
    flags[0:SPAN] = jnp.zeros((SPAN,) + flags.shape[1:], F32)

    cell_row = lax.broadcasted_iota(jnp.int32, (CELLS, 4 * LANES), 0)
    lane = lax.broadcasted_iota(jnp.int32, (CELLS, 4 * LANES), 1)
    pick = lax.rem(lane, LANES) // ML_RG == cell_row
    sum_re = jnp.where(pick, 1.0, 0.0).astype(BF16)
    sum_im = jnp.where(pick, jnp.where(lax.rem(lane, 2 * LANES) < LANES, -1.0, 1.0), 0.0).astype(BF16)
    contract = (((1,), (1,)), ((), ()))

    def looks(value, selector):
        high = value.astype(BF16)
        low = (value - high.astype(F32)).astype(BF16)
        both = jnp.concatenate([high, low], axis=1)
        return lax.dot_general(selector, both, contract, preferred_element_type=F32)

    ring = bands.shape[0]

    group = 4 if n % 4 == 0 else 1

    def some_dates(strip, i):
        r0, r1 = cuts[strip], cuts[strip + 1]
        first = max(r0 - ML_AZ, 0)
        b0 = first // ML_AZ
        count = (r1 - first) // ML_AZ - 1
        pad = -(-count // 8) * 8
        base = first // 16 * 16
        off = first - base
        high_rows = r1 - base
        for u in range(group):
            d = i * group + u
            pltpu.make_async_copy(
                strip_of(recv.at[d], strip), strip_of(recv.at[d], strip), recv_sem.at[strip, d]
            ).wait()
            if strip == 0:
                pltpu.make_async_copy(
                    flags.at[d + SPAN], flags.at[d + SPAN], frecv_sem.at[d]
                ).wait()
        pieces_in = [recv[i * group + u, base:r1] for u in range(group)]
        made = jnp.dot(
            jnp.concatenate(pieces_in, axis=0), mat[...], preferred_element_type=F32
        )
        for g in range(8):
            filt[g, 0:group * high_rows, :] = made[:, g * LANES:g * LANES + LANES]
        for u in range(group):
            slot = lax.rem(i * group + u, ring)
            for r in range(ML_AZ):
                for g in range(4):
                    start = u * high_rows + off + r
                    low = filt[g, pl.ds(start, count, stride=ML_AZ), :]
                    high = filt[g + 4, pl.ds(start + ML_AZ, count, stride=ML_AZ), :]
                    value = (low + high).astype(BF16).astype(F32)
                    bands[slot, r, 0:count, g * LANES:g * LANES + LANES] = value
        for u in range(group):
            d = i * group + u
            slot = lax.rem(d, ring)
            re_list = []
            im_list = []
            for band in range(2):
                cols = slice(band * 256, band * 256 + 256)
                for k in range(SPAN + 1):
                    early = lax.rem(d + ring - k, ring)
                    total_re = None
                    total_im = None
                    for r in range(ML_AZ):
                        a = bands[early, r, 0:pad, cols]
                        b = bands[slot, r, 0:pad, cols]
                        total_re = a * b if r == 0 else total_re + a * b
                        if k > 0:
                            b_swap = jnp.concatenate([b[:, 128:], b[:, :128]], axis=1)
                            total_im = a * b_swap if r == 0 else total_im + a * b_swap
                    re_list.append(total_re)
                    if k > 0:
                        im_list.append(total_im)
            re_looks = looks(jnp.concatenate(re_list, axis=0), sum_re)
            im_looks = looks(jnp.concatenate(im_list, axis=0), sum_im)
            for band in range(2):
                at = band * (SPAN + 1) * pad
                power[band, d + SPAN, :, b0:b0 + count] = re_looks[:, at:at + count]
                for k in range(1, SPAN + 1):
                    at = (band * (SPAN + 1) + k) * pad
                    cross[k - 1, 2 * band, d - k + SPAN, :, b0:b0 + count] = re_looks[:, at:at + count]
                    at = (band * SPAN + k - 1) * pad
                    cross[k - 1, 2 * band + 1, d - k + SPAN, :, b0:b0 + count] = im_looks[:, at:at + count]

    for strip in range(2):

        def step_dates(i, carry):
            some_dates(strip, i)
            return carry

        lax.fori_loop(0, n // group, step_dates, 0)

    step = min(8, n)
    shape = (step, CELLS, LANES)
    c_id = lax.broadcasted_iota(jnp.int32, shape, 1)
    b_id = lax.broadcasted_iota(jnp.int32, shape, 2)
    cell = CELLS * (own_blocks * my_q - 2 + b_id) + 1 + c_id
    valid = (b_id < blocks) & (cell >= 0) & (cell < n_rg * own_blocks * CELLS)

    def box(value):
        value = jnp.where(valid, value, 0.0)
        prefix = value
        for hop in (1, 2, 4):
            prefix = prefix + jnp.where(c_id >= hop, pltpu.roll(prefix, hop, 1), 0.0)
        whole = jnp.sum(value, axis=1, keepdims=True)
        suffix = whole - prefix + value
        return pltpu.roll(suffix, 1, 2) + whole + pltpu.roll(prefix, LANES - 1, 2)

    f_lane = lax.broadcasted_iota(jnp.int32, (step, 1, LANES), 2)

    def smooth(i, carry):
        at = i * step + SPAN
        for k in range(SPAN):
            cr0, ci0, cr1, ci1 = (cross[k, m, pl.ds(at, step)] for m in range(4))
            ab0 = power[0, pl.ds(at, step)] * power[0, pl.ds(at + k + 1, step)] + eps_power
            ab1 = power[1, pl.ds(at, step)] * power[1, pl.ds(at + k + 1, step)] + eps_power
            flag = jnp.sum(jnp.where(f_lane == k, flags[pl.ds(at, step)], 0.0), axis=2, keepdims=True)
            weight = flag * 0.5 * ((cr0 * cr0 + ci0 * ci0) / ab0 + (cr1 * cr1 + ci1 * ci1) / ab1)
            phase = split_coef * (ci0 * cr1 - cr0 * ci1) / jnp.sqrt(ab0 * ab1)
            den = box(weight)
            num = box(weight * phase)
            phs[k, pl.ds(at, step)] = num / (den + floor_weight)
            wgt[k, pl.ds(at, step)] = den / (2 * RADIUS + 1)
        return carry

    lax.fori_loop(0, n // step, smooth, 0)

    def chain(d, state):
        phi_a[d + SPAN] = state
        return state + phs[0, d + SPAN]

    lax.fori_loop(0, n, chain, jnp.zeros((CELLS, LANES), F32))

    def constants(i, carry):
        at = i * step + SPAN
        total = jnp.zeros(shape, F32)
        acc = ridge_weight * phi_a[pl.ds(at, step)]
        for k in range(1, SPAN + 1):
            w = wgt[k - 1, pl.ds(at, step)]
            low = wgt[k - 1, pl.ds(at - k, step)]
            total = total + w + low
            acc = acc - w * phs[k - 1, pl.ds(at, step)] + low * phs[k - 1, pl.ds(at - k, step)]
        wsum[pl.ds(i * step, step)] = total
        rhs[pl.ds(i * step, step)] = acc
        inv[pl.ds(i * step, step)] = 1.0 / (total + ridge_weight)
        return carry

    lax.fori_loop(0, n // step, constants, 0)

    for sweep in range(ITERS):
        old, new = (phi_a, phi_b) if sweep % 2 == 0 else (phi_b, phi_a)

        def relax(i, carry):
            at = i * step + SPAN
            acc = rhs[pl.ds(i * step, step)]
            for k in range(1, SPAN + 1):
                acc = acc + wgt[k - 1, pl.ds(at, step)] * old[pl.ds(at + k, step)]
                acc = acc + wgt[k - 1, pl.ds(at - k, step)] * old[pl.ds(at - k, step)]
            new[pl.ds(at, step)] = acc * inv[pl.ds(i * step, step)]
            return carry

        lax.fori_loop(0, n // step, relax, 0)
    last = phi_a if ITERS % 2 == 0 else phi_b

    def align(value):
        down = pltpu.roll(value, 1, 1)
        return jnp.where(c_id == 0, pltpu.roll(down, LANES - 1, 2), pltpu.roll(down, LANES - 2, 2))

    def finish(i, carry):
        phase = align(last[pl.ds(i * step + SPAN, step)])
        total = align(wsum[pl.ds(i * step, step)])
        pack[pl.ds(i * step, step)] = jnp.where(b_id < 64, phase, pltpu.roll(total, 64, 2))
        return carry

    lax.fori_loop(0, n // step, finish, 0)

    def out_copy(target):
        return pltpu.make_async_remote_copy(
            src_ref=pack.at[target], dst_ref=back.at[me],
            send_sem=osend_sem.at[target], recv_sem=orecv_sem.at[me],
            device_id={"date": target}, device_id_type=pl.DeviceIdType.MESH,
        )

    own_back = pltpu.make_async_copy(pack.at[me], back.at[me], orecv_sem.at[me])
    own_back.start()

    def send_back(i, carry):
        out_copy(lax.rem(me + i, n)).start()
        return carry

    lax.fori_loop(1, n, send_back, 0)

    def drain(i, carry):
        target = lax.rem(me + i, n)
        data_copy(target, 0).wait_send()
        data_copy(target, 1).wait_send()
        flag_copy(target).wait_send()
        out_copy(target).wait_send()
        return carry

    lax.fori_loop(1, n, drain, 0)

    def arrive(s, carry):
        pltpu.make_async_copy(back.at[s], back.at[s], orecv_sem.at[s]).wait()
        return carry

    lax.fori_loop(0, n, arrive, 0)

    wide = own_blocks * CELLS
    value = back[...].reshape(n * CELLS, LANES)
    high = value.astype(BF16)
    rest = value - high.astype(F32)
    middle = rest.astype(BF16)
    low = (rest - middle.astype(F32)).astype(BF16)
    place_row = lax.broadcasted_iota(jnp.int32, (LANES, 2 * wide), 0)
    place_col = lax.broadcasted_iota(jnp.int32, (LANES, 2 * wide), 1)
    place_row_of = (place_col // wide) * 64 + lax.rem(place_col, wide) // CELLS
    place = jnp.where(place_row == place_row_of, 1.0, 0.0).astype(BF16)
    spread = jnp.dot(
        jnp.concatenate([high, middle, low], axis=0), place, preferred_element_type=F32
    )
    count = n * CELLS
    spread = spread[0:count] + spread[count:2 * count] + spread[2 * count:3 * count]
    spread = spread.reshape(n, CELLS, 2 * wide)
    s_row = lax.broadcasted_iota(jnp.int32, spread.shape, 1)
    s_col = lax.broadcasted_iota(jnp.int32, spread.shape, 2)
    rows = jnp.sum(jnp.where(lax.rem(s_col, CELLS) == s_row, spread, 0.0), axis=1)
    for s in range(n):
        az, q = s // n_rg, s % n_rg
        phase_out[az:az + 1, q * wide:q * wide + wide] = rows[s:s + 1, 0:wide]
        total_out[az:az + 1, q * wide:q * wide + wide] = rows[s:s + 1, wide:2 * wide]


def local(slc_stack, band_taps, pair_flags):
    n = lax.axis_size("date")
    rows, span = slc_stack.shape[2:]
    n_az = rows // ML_AZ
    n_rg = n // n_az
    own_blocks = span // LANES // n_rg
    pieces = own_blocks + 4
    rows_pad = -(-(pieces - 1) // 8) * 8
    chunk_rows = ML_AZ * pieces

    half = -(-chunk_rows // 32) * 16
    cuts = (0, half, chunk_rows)
    padded_rows = ML_AZ * (span // LANES + 4)

    vmem = pl.BlockSpec(memory_space=pltpu.VMEM)
    small = lambda *lead: pltpu.VMEM((*lead, CELLS, LANES), F32)
    ring = 2 * SPAN
    sem = pltpu.SemaphoreType.DMA((n,))
    two_sem = pltpu.SemaphoreType.DMA((2, n))
    phase, total = pl.pallas_call(
        functools.partial(kernel, n, n_rg, pieces, cuts),
        out_shape=[jax.ShapeDtypeStruct((n_az, span // ML_RG), F32)] * 2,
        in_specs=[pl.BlockSpec(memory_space=pl.ANY)] * 3,
        out_specs=[vmem] * 2,
        scratch_shapes=[
            pltpu.VMEM((2, rows, span), BF16),
            pltpu.VMEM((1, SPAN), jnp.int32),
            pltpu.VMEM((2, 2, TAPS), BF16),
            pltpu.VMEM((8, LANES), F32),
            pltpu.VMEM((n_az, padded_rows, 2 * LANES), BF16),
            pltpu.VMEM((1, LANES), F32),
            pltpu.VMEM((n, chunk_rows, 2 * LANES), BF16),
            pltpu.VMEM((n + SPAN, 1, LANES), F32),
            pltpu.VMEM((256, 1024), BF16),
            pltpu.VMEM((8, 4 * chunk_rows, LANES), F32),
            pltpu.VMEM((ring, ML_AZ, rows_pad, 512), F32),
            small(2, n + 2 * SPAN),
            small(SPAN, 4, n + 2 * SPAN),
            small(SPAN, n + 2 * SPAN),
            small(SPAN, n + 2 * SPAN),
            small(n + 2 * SPAN),
            small(n + 2 * SPAN),
            small(n),
            small(n),
            small(n),
            small(n),
            small(n),
            pltpu.SemaphoreType.DMA((3,)), two_sem, two_sem, sem, sem, sem, sem,
        ],
        compiler_params=pltpu.CompilerParams(
            collective_id=0, has_side_effects=True, vmem_limit_bytes=60 * 1024 * 1024
        ),
    )(slc_stack, pair_flags, band_taps)
    return phase[None], total[None]


def solution(mesh):
    in_specs = (P("date", None, "group", None), P(), P("date", None))
    out_specs = (P("date", "group", None), P("date", "group", None))
    return jax.shard_map(local, mesh=mesh, in_specs=in_specs, out_specs=out_specs, check_vma=False)
```

```python
import functools

import jax
import jax.numpy as jnp
from jax import lax
from jax.experimental import pallas as pl
from jax.experimental.pallas import tpu as pltpu
from jax.sharding import PartitionSpec as P

TAPS = 32
ML_AZ = 4
ML_RG = 16
SPAN = 4
RADIUS = 8
ITERS = 4

LANES = 128
CELLS = LANES // ML_RG

eps_power = 1e-06
floor_weight = 0.1
ridge_weight = 0.05
split_coef = 2.0

F32 = jnp.float32
BF16 = jnp.bfloat16


def kernel(
    n, n_rg, pieces, cuts,
    slc_hbm, flags_hbm, taps_hbm, out_ref,
    slc, flags_in, taps_in, taps_ref, data, own_flags, recv, flags, mat, filt, bands, power, cross, wgt, phs, phi_a, phi_b,
    rhs, inv, wsum, pack, back,
    in_sem, send_sem, recv_sem, fsend_sem, frecv_sem, osend_sem, orecv_sem,
):
    me = lax.axis_index("date")
    blocks = pieces - 1
    own_blocks = pieces - 4
    rows_pad = bands.shape[2]
    my_q = lax.rem(me, n_rg)

    slc_load = pltpu.make_async_copy(slc_hbm.at[0], slc, in_sem.at[0])
    slc_load.start()
    flags_load = pltpu.make_async_copy(flags_hbm, flags_in, in_sem.at[1])
    flags_load.start()
    taps_load = pltpu.make_async_copy(taps_hbm, taps_in, in_sem.at[2])
    taps_load.start()
    barrier = pltpu.get_barrier_semaphore()

    def greet(i, carry):
        other = lax.rem(me + i, n)
        pl.semaphore_signal(
            barrier, inc=1, device_id={"date": other}, device_id_type=pl.DeviceIdType.MESH
        )
        return carry

    lax.fori_loop(1, n, greet, 0)

    flags_load.wait()
    own_flags[...] = jnp.zeros_like(own_flags)
    own_flags[0:1, 0:SPAN] = flags_in[...].astype(F32)
    taps_load.wait()
    taps_ref[...] = jnp.zeros_like(taps_ref)
    for band in range(2):
        taps_ref[2 * band:2 * band + 2, 0:TAPS] = taps_in[band].astype(F32)
    slc_load.wait()

    n_az = n // n_rg
    n_tiles = data.shape[1] // 16
    n_blocks = slc.shape[2] // LANES
    upper = lax.broadcasted_iota(jnp.int32, (8, LANES), 0) < ML_AZ

    def regroup(tile, lo, hi):
        for part in range(2):
            for half in range(n_az // 2):
                made = ([], [])
                for pair in range(2):
                    two = []
                    for m in (2 * pair, 2 * pair + 1):
                        if lo <= m < hi:
                            at = pl.multiple_of((4 * tile - 2 + m) * LANES, LANES)
                            value = slc[part, :, pl.ds(at, LANES)].astype(F32)
                            two.append(value[8 * half:8 * half + 8])
                        else:
                            two.append(jnp.zeros((8, LANES), F32))
                    made[0].append(jnp.where(upper, two[0], pltpu.roll(two[1], ML_AZ, 0)))
                    made[1].append(jnp.where(upper, pltpu.roll(two[0], ML_AZ, 0), two[1]))
                for odd in range(2):
                    value = jnp.concatenate(made[odd], axis=0).astype(BF16)
                    to = pl.multiple_of(tile * 16, 16)
                    data[2 * half + odd, pl.ds(to, 16), part * LANES:part * LANES + LANES] = value

    def inner_tile(tile, carry):
        regroup(tile, 0, 4)
        return carry

    lax.fori_loop(1, n_tiles - 1, inner_tile, 0, unroll=False)
    regroup(0, 2, 4)
    regroup(n_tiles - 1, 0, 2)

    chunk_rows = ML_AZ * pieces
    stride_rows = ML_AZ * own_blocks

    def strip_of(ref, strip):
        lo, hi = cuts[strip], cuts[strip + 1]
        return ref.at[pl.ds(lo, hi - lo)]

    def source(target, strip):
        lo, hi = cuts[strip], cuts[strip + 1]
        begin = pl.multiple_of(lax.rem(target, n_rg) * stride_rows + lo, 16)
        return data.at[target // n_rg, pl.ds(begin, hi - lo)]

    def data_copy(target, strip):
        return pltpu.make_async_remote_copy(
            src_ref=source(target, strip), dst_ref=strip_of(recv.at[me], strip),
            send_sem=send_sem.at[strip, target], recv_sem=recv_sem.at[strip, me],
            device_id={"date": target}, device_id_type=pl.DeviceIdType.MESH,
        )

    def flag_copy(target):
        return pltpu.make_async_remote_copy(
            src_ref=own_flags, dst_ref=flags.at[me + SPAN],
            send_sem=fsend_sem.at[target], recv_sem=frecv_sem.at[me],
            device_id={"date": target}, device_id_type=pl.DeviceIdType.MESH,
        )

    for strip in range(2):
        pltpu.make_async_copy(
            source(me, strip), strip_of(recv.at[me], strip), recv_sem.at[strip, me]
        ).start()
    pltpu.make_async_copy(own_flags, flags.at[me + SPAN], frecv_sem.at[me]).start()

    pl.semaphore_wait(barrier, n - 1)

    def send_strip(strip):
        def send_pair(i, carry):
            for target, go in ((n - 1 - i, n - 1 - i > me), (i, i < me)):
                @pl.when(go)
                def _():
                    data_copy(target, strip).start()
                    if strip == 0:
                        flag_copy(target).start()
            return carry

        lax.fori_loop(0, n, send_pair, 0)

    send_strip(0)
    send_strip(1)

    k_id = lax.broadcasted_iota(jnp.int32, (LANES, LANES), 0)
    j_id = lax.broadcasted_iota(jnp.int32, (LANES, LANES), 1)
    circ = []
    for m in range(4):
        base = jnp.broadcast_to(taps_ref[m:m + 1, :], (LANES, LANES))
        circ.append(pltpu.roll(base, 0, 1, stride=1, stride_axis=0).T)
    for half in range(2):
        keep = (j_id <= k_id) if half == 0 else (j_id > k_id)
        for band in range(2):
            re_part = jnp.where(keep, circ[2 * band], 0.0).astype(BF16)
            im_value = jnp.where(keep, circ[2 * band + 1], 0.0)
            im_part = im_value.astype(BF16)
            im_minus = (-im_value).astype(BF16)
            col = half * 512 + band * 256
            mat[0:128, col:col + 128] = re_part
            mat[0:128, col + 128:col + 256] = im_part
            mat[128:256, col:col + 128] = im_minus
            mat[128:256, col + 128:col + 256] = re_part

    for ref in (bands, power, cross, wgt, phs, phi_a, phi_b):
        ref[...] = jnp.zeros_like(ref)
    flags[0:SPAN] = jnp.zeros((SPAN,) + flags.shape[1:], F32)

    cell_row = lax.broadcasted_iota(jnp.int32, (CELLS, 4 * LANES), 0)
    lane = lax.broadcasted_iota(jnp.int32, (CELLS, 4 * LANES), 1)
    pick = lax.rem(lane, LANES) // ML_RG == cell_row
    sum_re = jnp.where(pick, 1.0, 0.0).astype(BF16)
    sum_im = jnp.where(pick, jnp.where(lax.rem(lane, 2 * LANES) < LANES, -1.0, 1.0), 0.0).astype(BF16)
    contract = (((1,), (1,)), ((), ()))

    def looks(value, selector):
        high = value.astype(BF16)
        low = (value - high.astype(F32)).astype(BF16)
        both = jnp.concatenate([high, low], axis=1)
        return lax.dot_general(selector, both, contract, preferred_element_type=F32)

    ring = bands.shape[0]

    group = 4 if n % 4 == 0 else 1

    def some_dates(strip, i):
        r0, r1 = cuts[strip], cuts[strip + 1]
        first = max(r0 - ML_AZ, 0)
        b0 = first // ML_AZ
        count = (r1 - first) // ML_AZ - 1
        pad = -(-count // 8) * 8
        base = first // 16 * 16
        off = first - base
        high_rows = r1 - base
        for u in range(group):
            d = i * group + u
            pltpu.make_async_copy(
                strip_of(recv.at[d], strip), strip_of(recv.at[d], strip), recv_sem.at[strip, d]
            ).wait()
            if strip == 0:
                pltpu.make_async_copy(
                    flags.at[d + SPAN], flags.at[d + SPAN], frecv_sem.at[d]
                ).wait()
        pieces_in = [recv[i * group + u, base:r1] for u in range(group)]
        made = jnp.dot(
            jnp.concatenate(pieces_in, axis=0), mat[...], preferred_element_type=F32
        )
        for g in range(8):
            filt[g, 0:group * high_rows, :] = made[:, g * LANES:g * LANES + LANES]
        for u in range(group):
            slot = lax.rem(i * group + u, ring)
            for r in range(ML_AZ):
                for g in range(4):
                    start = u * high_rows + off + r
                    low = filt[g, pl.ds(start, count, stride=ML_AZ), :]
                    high = filt[g + 4, pl.ds(start + ML_AZ, count, stride=ML_AZ), :]
                    value = (low + high).astype(BF16).astype(F32)
                    bands[slot, r, 0:count, g * LANES:g * LANES + LANES] = value
        for u in range(group):
            d = i * group + u
            slot = lax.rem(d, ring)
            re_list = []
            im_list = []
            for band in range(2):
                cols = slice(band * 256, band * 256 + 256)
                for k in range(SPAN + 1):
                    early = lax.rem(d + ring - k, ring)
                    total_re = None
                    total_im = None
                    for r in range(ML_AZ):
                        a = bands[early, r, 0:pad, cols]
                        b = bands[slot, r, 0:pad, cols]
                        total_re = a * b if r == 0 else total_re + a * b
                        if k > 0:
                            b_swap = jnp.concatenate([b[:, 128:], b[:, :128]], axis=1)
                            total_im = a * b_swap if r == 0 else total_im + a * b_swap
                    re_list.append(total_re)
                    if k > 0:
                        im_list.append(total_im)
            re_looks = looks(jnp.concatenate(re_list, axis=0), sum_re)
            im_looks = looks(jnp.concatenate(im_list, axis=0), sum_im)
            for band in range(2):
                at = band * (SPAN + 1) * pad
                power[band, d + SPAN, :, b0:b0 + count] = re_looks[:, at:at + count]
                for k in range(1, SPAN + 1):
                    at = (band * (SPAN + 1) + k) * pad
                    cross[k - 1, 2 * band, d - k + SPAN, :, b0:b0 + count] = re_looks[:, at:at + count]
                    at = (band * SPAN + k - 1) * pad
                    cross[k - 1, 2 * band + 1, d - k + SPAN, :, b0:b0 + count] = im_looks[:, at:at + count]

    for strip in range(2):

        def step_dates(i, carry):
            some_dates(strip, i)
            return carry

        lax.fori_loop(0, n // group, step_dates, 0)

    step = min(8, n)
    shape = (step, CELLS, LANES)
    c_id = lax.broadcasted_iota(jnp.int32, shape, 1)
    b_id = lax.broadcasted_iota(jnp.int32, shape, 2)
    cell = CELLS * (own_blocks * my_q - 2 + b_id) + 1 + c_id
    valid = (b_id < blocks) & (cell >= 0) & (cell < n_rg * own_blocks * CELLS)

    def box(value):
        value = jnp.where(valid, value, 0.0)
        prefix = value
        for hop in (1, 2, 4):
            prefix = prefix + jnp.where(c_id >= hop, pltpu.roll(prefix, hop, 1), 0.0)
        whole = jnp.sum(value, axis=1, keepdims=True)
        suffix = whole - prefix + value
        return pltpu.roll(suffix, 1, 2) + whole + pltpu.roll(prefix, LANES - 1, 2)

    f_lane = lax.broadcasted_iota(jnp.int32, (step, 1, LANES), 2)

    def smooth(i, carry):
        at = i * step + SPAN
        for k in range(SPAN):
            cr0, ci0, cr1, ci1 = (cross[k, m, pl.ds(at, step)] for m in range(4))
            ab0 = power[0, pl.ds(at, step)] * power[0, pl.ds(at + k + 1, step)] + eps_power
            ab1 = power[1, pl.ds(at, step)] * power[1, pl.ds(at + k + 1, step)] + eps_power
            flag = jnp.sum(jnp.where(f_lane == k, flags[pl.ds(at, step)], 0.0), axis=2, keepdims=True)
            weight = flag * 0.5 * ((cr0 * cr0 + ci0 * ci0) / ab0 + (cr1 * cr1 + ci1 * ci1) / ab1)
            phase = split_coef * (ci0 * cr1 - cr0 * ci1) / jnp.sqrt(ab0 * ab1)
            den = box(weight)
            num = box(weight * phase)
            phs[k, pl.ds(at, step)] = num / (den + floor_weight)
            wgt[k, pl.ds(at, step)] = den / (2 * RADIUS + 1)
        return carry

    lax.fori_loop(0, n // step, smooth, 0)

    def chain(d, state):
        phi_a[d + SPAN] = state
        return state + phs[0, d + SPAN]

    lax.fori_loop(0, n, chain, jnp.zeros((CELLS, LANES), F32))

    def constants(i, carry):
        at = i * step + SPAN
        total = jnp.zeros(shape, F32)
        acc = ridge_weight * phi_a[pl.ds(at, step)]
        for k in range(1, SPAN + 1):
            w = wgt[k - 1, pl.ds(at, step)]
            low = wgt[k - 1, pl.ds(at - k, step)]
            total = total + w + low
            acc = acc - w * phs[k - 1, pl.ds(at, step)] + low * phs[k - 1, pl.ds(at - k, step)]
        wsum[pl.ds(i * step, step)] = total
        rhs[pl.ds(i * step, step)] = acc
        inv[pl.ds(i * step, step)] = 1.0 / (total + ridge_weight)
        return carry

    lax.fori_loop(0, n // step, constants, 0)

    for sweep in range(ITERS):
        old, new = (phi_a, phi_b) if sweep % 2 == 0 else (phi_b, phi_a)

        def relax(i, carry):
            at = i * step + SPAN
            acc = rhs[pl.ds(i * step, step)]
            for k in range(1, SPAN + 1):
                acc = acc + wgt[k - 1, pl.ds(at, step)] * old[pl.ds(at + k, step)]
                acc = acc + wgt[k - 1, pl.ds(at - k, step)] * old[pl.ds(at - k, step)]
            new[pl.ds(at, step)] = acc * inv[pl.ds(i * step, step)]
            return carry

        lax.fori_loop(0, n // step, relax, 0)
    last = phi_a if ITERS % 2 == 0 else phi_b

    def align(value):
        down = pltpu.roll(value, 1, 1)
        return jnp.where(c_id == 0, pltpu.roll(down, LANES - 1, 2), pltpu.roll(down, LANES - 2, 2))

    def finish(i, carry):
        phase = align(last[pl.ds(i * step + SPAN, step)])
        total = align(wsum[pl.ds(i * step, step)])
        pack[pl.ds(i * step, step)] = jnp.where(b_id < 64, phase, pltpu.roll(total, 64, 2))
        return carry

    lax.fori_loop(0, n // step, finish, 0)

    def out_copy(target):
        return pltpu.make_async_remote_copy(
            src_ref=pack.at[target], dst_ref=back.at[me],
            send_sem=osend_sem.at[target], recv_sem=orecv_sem.at[me],
            device_id={"date": target}, device_id_type=pl.DeviceIdType.MESH,
        )

    own_back = pltpu.make_async_copy(pack.at[me], back.at[me], orecv_sem.at[me])
    own_back.start()

    def send_back(i, carry):
        out_copy(lax.rem(me + i, n)).start()
        return carry

    lax.fori_loop(1, n, send_back, 0)

    def drain(i, carry):
        target = lax.rem(me + i, n)
        data_copy(target, 0).wait_send()
        data_copy(target, 1).wait_send()
        flag_copy(target).wait_send()
        out_copy(target).wait_send()
        return carry

    lax.fori_loop(1, n, drain, 0)

    def arrive(s, carry):
        pltpu.make_async_copy(back.at[s], back.at[s], orecv_sem.at[s]).wait()
        return carry

    lax.fori_loop(0, n, arrive, 0)

    wide = own_blocks * CELLS
    value = back[...].reshape(n * CELLS, LANES)
    high = value.astype(BF16)
    rest = value - high.astype(F32)
    middle = rest.astype(BF16)
    low = (rest - middle.astype(F32)).astype(BF16)
    place_row = lax.broadcasted_iota(jnp.int32, (LANES, 2 * wide), 0)
    place_col = lax.broadcasted_iota(jnp.int32, (LANES, 2 * wide), 1)
    place_row_of = (place_col // wide) * 64 + lax.rem(place_col, wide) // CELLS
    place = jnp.where(place_row == place_row_of, 1.0, 0.0).astype(BF16)
    spread = jnp.dot(
        jnp.concatenate([high, middle, low], axis=0), place, preferred_element_type=F32
    )
    count = n * CELLS
    spread = spread[0:count] + spread[count:2 * count] + spread[2 * count:3 * count]
    spread = spread.reshape(n, CELLS, 2 * wide)
    s_row = lax.broadcasted_iota(jnp.int32, spread.shape, 1)
    s_col = lax.broadcasted_iota(jnp.int32, spread.shape, 2)
    rows = jnp.sum(jnp.where(lax.rem(s_col, CELLS) == s_row, spread, 0.0), axis=1)
    for s in range(n):
        az, q = s // n_rg, s % n_rg
        out_ref[0, az:az + 1, q * wide:q * wide + wide] = rows[s:s + 1, 0:wide]
        out_ref[1, az:az + 1, q * wide:q * wide + wide] = rows[s:s + 1, wide:2 * wide]


def local(slc_stack, band_taps, pair_flags):
    n = lax.axis_size("date")
    rows, span = slc_stack.shape[2:]
    n_az = rows // ML_AZ
    n_rg = n // n_az
    own_blocks = span // LANES // n_rg
    pieces = own_blocks + 4
    rows_pad = -(-(pieces - 1) // 8) * 8
    chunk_rows = ML_AZ * pieces

    half = -(-chunk_rows // 32) * 16
    cuts = (0, half, chunk_rows)
    padded_rows = ML_AZ * (span // LANES + 4)

    vmem = pl.BlockSpec(memory_space=pltpu.VMEM)
    small = lambda *lead: pltpu.VMEM((*lead, CELLS, LANES), F32)
    ring = 2 * SPAN
    sem = pltpu.SemaphoreType.DMA((n,))
    two_sem = pltpu.SemaphoreType.DMA((2, n))
    both = pl.pallas_call(
        functools.partial(kernel, n, n_rg, pieces, cuts),
        out_shape=jax.ShapeDtypeStruct((2, n_az, span // ML_RG), F32),
        in_specs=[pl.BlockSpec(memory_space=pl.ANY)] * 3,
        out_specs=vmem,
        scratch_shapes=[
            pltpu.VMEM((2, rows, span), BF16),
            pltpu.VMEM((1, SPAN), jnp.int32),
            pltpu.VMEM((2, 2, TAPS), BF16),
            pltpu.VMEM((8, LANES), F32),
            pltpu.VMEM((n_az, padded_rows, 2 * LANES), BF16),
            pltpu.VMEM((1, LANES), F32),
            pltpu.VMEM((n, chunk_rows, 2 * LANES), BF16),
            pltpu.VMEM((n + SPAN, 1, LANES), F32),
            pltpu.VMEM((256, 1024), BF16),
            pltpu.VMEM((8, 4 * chunk_rows, LANES), F32),
            pltpu.VMEM((ring, ML_AZ, rows_pad, 512), F32),
            small(2, n + 2 * SPAN),
            small(SPAN, 4, n + 2 * SPAN),
            small(SPAN, n + 2 * SPAN),
            small(SPAN, n + 2 * SPAN),
            small(n + 2 * SPAN),
            small(n + 2 * SPAN),
            small(n),
            small(n),
            small(n),
            small(n),
            small(n),
            pltpu.SemaphoreType.DMA((3,)), two_sem, two_sem, sem, sem, sem, sem,
        ],
        compiler_params=pltpu.CompilerParams(
            collective_id=0, has_side_effects=True, vmem_limit_bytes=60 * 1024 * 1024
        ),
    )(slc_stack, pair_flags, band_taps)
    return both[0:1], both[1:2]


def solution(mesh):
    in_specs = (P("date", None, "group", None), P(), P("date", None))
    out_specs = (P("date", "group", None), P("date", "group", None))
    return jax.shard_map(local, mesh=mesh, in_specs=in_specs, out_specs=out_specs, check_vma=False)
```
